32 devices in a mesh: clip: 2 (over x), frame: 8 (over z, y), band: 2 (over core).
Axes of the slice: x: 2, y: 2, z: 4, core: 2. Of those that a mesh axis runs over, the one named last changes fastest.
Arguments:
- pixels: bfloat16 [16, 16, 32, 256], P(('clip', 'frame'), 'band'), parts along dimension 0, may hold values from -40 to 40
- gru_state: bfloat16 [16, 16, 32, 128], P(('clip', 'frame'), 'band'), parts along dimension 0, may hold values from -1 to 1
- tokens: bfloat16 [16, 1024, 256], P(('clip', 'frame'), 'band'), parts along dimension 0, may hold values from -30 to 30
- visible: int32 [16, 1024], P(('clip', 'frame'), 'band'), parts along dimension 0, may hold values from 0 to 1, as said below
- query_frame: int32 [2048], P(('clip', 'band')), parts along dimension 0, may hold values from 0 to 7, as said below
- pixel_query: bfloat16 [256, 256], replicated, may hold values from -2 to 2
- pixel_key: bfloat16 [256, 256], replicated, may hold values from -2 to 2
- pixel_value: bfloat16 [256, 256], replicated, may hold values from -0.375 to 0.375
- pixel_out: bfloat16 [256, 128], replicated, may hold values from -1.5 to 1.5
- time_query: bfloat16 [256, 256], replicated, may hold values from -2 to 2
- time_key: bfloat16 [256, 256], replicated, may hold values from -2 to 2
- time_value: bfloat16 [256, 256], replicated, may hold values from -0.375 to 0.375
- time_out: bfloat16 [256, 256], replicated, may hold values from -0.75 to 0.75
- gru_gates: bfloat16 [3, 3, 256, 256], replicated, may hold values from -0.125 to 0.125
- gru_candidate: bfloat16 [3, 3, 256, 128], replicated, may hold values from -0.125 to 0.125
Outputs:
- refined_state: bfloat16 [16, 16, 32, 128], P(('clip', 'frame'), 'band'), parts along dimension 0
- track_out: bfloat16 [16, 1024, 256], P(('clip', 'frame'), 'band'), parts along dimension 0
The draws below stay inside these ranges and needn't reach their ends.
There are 2 independent parts, one for each index of `clip`. The reference program is written for one: setup_inputs(seed, part) draws one part's arguments, and reference() takes and returns one part's arrays. A program takes and returns all parts, laid end to end along the dimension named above; an argument that names none is the same for every part. Nothing has to cross between parts.
Inputs may be any that keep to these rules, and one draw needn't show every extreme that they name: Each track is visible in the frame named by its query frame index. `query_frame`: every frame is the query frame of exactly 128 tracks.
All inputs are finite; a program needn't handle non-finite values.
Results may differ from the reference program's by a relative error of at most 0.0095.
The reference program's roundings to bfloat16 on the way count: a program that leaves them out, or rounds other values in their place, can miss the bound.
Values may be sent and summed in bfloat16 or wider, within the bound.
A program may use at most 64 MiB of HBM per device.

```python
import math
import jax
import jax.numpy as jnp
from jax import lax

CHANNELS = 256
HEADS = 8
HEAD_DIM = 32
GRU_WIDTH = 128
TRACKS = 1024
WIDTH = 32
ITERS = 2
FRAMES = 8
ROWS = 16


def draw_pixels(key, part):
    full_shape = (FRAMES, ROWS, WIDTH, CHANNELS)
    drawn = jnp.clip(jax.random.normal(jax.random.fold_in(key, 502), full_shape, jnp.float32), -4.0, 4.0)
    return drawn.astype(jnp.bfloat16)


def draw_tokens(key, part):
    full_shape = (FRAMES, TRACKS, CHANNELS)
    drawn = jnp.clip(jax.random.normal(jax.random.fold_in(key, 506), full_shape, jnp.float32), -4.0, 4.0)
    return drawn.astype(jnp.bfloat16)


def track_layout(key):
    shuffled = jax.random.permutation(jax.random.fold_in(key, 701), TRACKS)
    anchor_frames = (shuffled % FRAMES).astype(jnp.int32)
    coin_flips = jax.random.randint(jax.random.fold_in(key, 702), (FRAMES, TRACKS), 0, 5)
    frame_ids = jnp.arange(FRAMES, dtype=jnp.int32)[:, None]
    seen_mask = jnp.logical_or(coin_flips < 3, frame_ids == anchor_frames[None, :]).astype(jnp.int32)
    return (seen_mask, anchor_frames)


def draw_visible(key, part):
    return track_layout(key)[0]


def draw_query_frame(key, part):
    return track_layout(key)[1]


def weight_pair(key, salt):
    first = jnp.clip(jax.random.normal(jax.random.fold_in(key, salt), (CHANNELS, CHANNELS), jnp.float32), -4.0, 4.0)
    second = jnp.clip(jax.random.normal(jax.random.fold_in(key, salt + 1), (CHANNELS, CHANNELS), jnp.float32), -4.0, 4.0)
    return (first, second)


def query_weight(key, salt):
    first, second = weight_pair(key, salt)
    return (2.0 * first / math.sqrt(CHANNELS)).astype(jnp.bfloat16)


def key_weight(key, salt):
    first, second = weight_pair(key, salt)
    mixed = second / math.sqrt(CHANNELS)
    return mixed.astype(jnp.bfloat16)


def draw_pixel_query(key, part):
    return query_weight(key, 601)


def draw_pixel_key(key, part):
    return key_weight(key, 601)


def draw_time_query(key, part):
    return query_weight(key, 611)


def draw_time_key(key, part):
    return key_weight(key, 611)


def block_levels(key, extent, shards, least, high):
    def one(dim, shards_of):
        steps = jax.random.uniform(jax.random.fold_in(jax.random.fold_in(key, 6), dim), (shards_of,), jnp.float32, least / len(shards), high / len(shards))
        return jnp.repeat(jnp.exp(steps), extent[dim] // shards_of).reshape((-1,) + (1,) * (len(extent) - dim - 1))

    loudness = one(*shards[0])
    for cut in shards[1:]:
        loudness = loudness * one(*cut)
    return loudness


def normal_values(rng, extent, spread, reach, held_as=jnp.bfloat16):
    values = jax.random.normal(rng, extent, jnp.float32) * spread
    return jnp.minimum(jnp.maximum(values, -reach), reach).astype(held_as)


def setup_inputs(seed: int = 0, part: int = 0) -> dict:
    seeds = jax.random.split(jax.random.key(seed), 16)
    own_keys = jax.random.split(jax.random.fold_in(seeds[15], part), 16)
    pixels = draw_pixels(jax.random.fold_in(jax.random.fold_in(seeds[15], part), 71), part)
    gru_state = jnp.clip(jax.random.uniform(own_keys[1], (FRAMES, ROWS, WIDTH, GRU_WIDTH), jnp.float32, -1.0, 1.0) * block_levels(own_keys[1], (FRAMES, ROWS, WIDTH, GRU_WIDTH), ((0, 8), (1, 2)), -0.4, 0.0), -1.0, 1.0).astype(jnp.bfloat16)
    tokens = draw_tokens(jax.random.fold_in(jax.random.fold_in(seeds[15], part), 71), part)
    visible = draw_visible(jax.random.fold_in(jax.random.fold_in(seeds[15], part), 71), part)
    query_frame = draw_query_frame(jax.random.fold_in(jax.random.fold_in(seeds[15], part), 71), part)
    pixel_query = draw_pixel_query(jax.random.fold_in(seeds[15], 71), part)
    pixel_key = draw_pixel_key(jax.random.fold_in(seeds[15], 71), part)
    pixel_value = normal_values(seeds[7], (CHANNELS, CHANNELS), CHANNELS ** -0.5, 0.375)
    pixel_out = normal_values(seeds[8], (CHANNELS, GRU_WIDTH), (CHANNELS // 16) ** -0.5, 1.5)
    time_query = draw_time_query(jax.random.fold_in(seeds[15], 71), part)
    time_key = draw_time_key(jax.random.fold_in(seeds[15], 71), part)
    time_value = normal_values(seeds[11], (CHANNELS, CHANNELS), CHANNELS ** -0.5, 0.375)
    time_out = normal_values(seeds[12], (CHANNELS, CHANNELS), (CHANNELS // 4) ** -0.5, 0.75)
    gru_gates = normal_values(seeds[13], (3, 3, 2 * GRU_WIDTH, 2 * GRU_WIDTH), (18 * GRU_WIDTH) ** -0.5, 0.125)
    gru_candidate = normal_values(seeds[14], (3, 3, 2 * GRU_WIDTH, GRU_WIDTH), (18 * GRU_WIDTH) ** -0.5, 0.125)
    return dict(pixels=pixels, gru_state=gru_state, tokens=tokens, visible=visible, query_frame=query_frame, pixel_query=pixel_query, pixel_key=pixel_key, pixel_value=pixel_value, pixel_out=pixel_out, time_query=time_query, time_key=time_key, time_value=time_value, time_out=time_out, gru_gates=gru_gates, gru_candidate=gru_candidate)


def attend_heads(queries, key_rows, value_rows, key_mask):
    score_scale = HEAD_DIM ** -0.5
    head_outputs = []
    for head_index in range(HEADS):
        offset = head_index * HEAD_DIM
        scores = jnp.dot(queries[:, offset:offset + HEAD_DIM], key_rows[:, offset:offset + HEAD_DIM].T, preferred_element_type=jnp.float32) * score_scale
        scores = jnp.where(key_mask[None, :], scores, -jnp.inf)
        weights = jax.nn.softmax(scores, axis=-1).astype(jnp.bfloat16)
        head_outputs.append(jnp.dot(weights, value_rows[:, offset:offset + HEAD_DIM], preferred_element_type=jnp.float32))
    return jnp.concatenate(head_outputs, axis=-1).astype(jnp.bfloat16)


def conv_rows(padded, weight, rows, columns):
    widened = jnp.pad(padded, ((0, 0), (1, 1), (0, 0)))
    summed = jnp.zeros((rows * columns, weight.shape[3]), jnp.float32)
    for row_shift in range(3):
        for col_shift in range(3):
            window = widened[row_shift:row_shift + rows, col_shift:col_shift + columns]
            summed = summed + jnp.dot(window.reshape(rows * columns, -1), weight[row_shift, col_shift], preferred_element_type=jnp.float32)
    return summed


def reference(pixels, gru_state, tokens, visible, query_frame, pixel_query, pixel_key, pixel_value, pixel_out, time_query, time_key, time_value, time_out, gru_gates, gru_candidate):
    def frame_context(inputs):
        frame_pixels, frame_tokens, frame_seen = inputs
        queries = jnp.dot(frame_pixels.reshape(ROWS * WIDTH, CHANNELS), pixel_query, preferred_element_type=jnp.float32).astype(jnp.bfloat16)
        key_rows = jnp.dot(frame_tokens, pixel_key, preferred_element_type=jnp.float32).astype(jnp.bfloat16)
        value_rows = jnp.dot(frame_tokens, pixel_value, preferred_element_type=jnp.float32).astype(jnp.bfloat16)
        attended = attend_heads(queries, key_rows, value_rows, frame_seen > 0)
        return jnp.dot(attended, pixel_out, preferred_element_type=jnp.float32).astype(jnp.bfloat16).reshape(ROWS, WIDTH, GRU_WIDTH)

    context = lax.map(frame_context, (pixels, tokens, visible))

    def frame_refine(inputs):
        state_now, context_now = inputs
        for iteration in range(ITERS):
            combined = jnp.concatenate([state_now, context_now], axis=-1)
            padded = jnp.pad(combined, ((1, 1), (0, 0), (0, 0)))
            gate_terms = conv_rows(padded, gru_gates, ROWS, WIDTH)
            update = jax.nn.sigmoid(gate_terms[:, :GRU_WIDTH])
            reset_gate = jax.nn.sigmoid(gate_terms[:, GRU_WIDTH:])
            state_flat = state_now.reshape(ROWS * WIDTH, GRU_WIDTH).astype(jnp.float32)
            reset_state = (reset_gate * state_flat).astype(jnp.bfloat16).reshape(ROWS, WIDTH, GRU_WIDTH)
            mixed_in = jnp.concatenate([reset_state, context_now], axis=-1)
            padded_mix = jnp.pad(mixed_in, ((1, 1), (0, 0), (0, 0)))
            candidate = jnp.tanh(conv_rows(padded_mix, gru_candidate, ROWS, WIDTH))
            state_now = ((1.0 - update) * state_flat + update * candidate).astype(jnp.bfloat16).reshape(ROWS, WIDTH, GRU_WIDTH)
        return state_now

    refined_state = lax.map(frame_refine, (gru_state, context))

    flat_tokens = tokens.reshape(FRAMES * TRACKS, CHANNELS)
    time_queries = jnp.dot(flat_tokens, time_query, preferred_element_type=jnp.float32).astype(jnp.bfloat16).reshape(FRAMES, TRACKS, CHANNELS)
    time_keys = jnp.dot(flat_tokens, time_key, preferred_element_type=jnp.float32).astype(jnp.bfloat16).reshape(FRAMES, TRACKS, CHANNELS)
    time_values = jnp.dot(flat_tokens, time_value, preferred_element_type=jnp.float32).astype(jnp.bfloat16).reshape(FRAMES, TRACKS, CHANNELS)
    anchor = time_queries[query_frame, jnp.arange(TRACKS)]
    joint_queries = (time_queries.astype(jnp.float32) + anchor.astype(jnp.float32)[None]).astype(jnp.bfloat16)
    shaped = (FRAMES, TRACKS, HEADS, HEAD_DIM)
    scores = jnp.einsum("fthd,gthd->thfg", joint_queries.astype(jnp.float32).reshape(shaped), time_keys.astype(jnp.float32).reshape(shaped)) * (HEAD_DIM ** -0.5)
    key_mask = jnp.transpose(visible) > 0
    scores = jnp.where(key_mask[:, None, None, :], scores, -jnp.inf)
    weights = jax.nn.softmax(scores, axis=-1).astype(jnp.bfloat16)
    attended = jnp.einsum("thfg,gthd->fthd", weights.astype(jnp.float32), time_values.astype(jnp.float32).reshape(shaped))
    time_attended = attended.astype(jnp.bfloat16).reshape(FRAMES * TRACKS, CHANNELS)
    projected = jnp.dot(time_attended, time_out, preferred_element_type=jnp.float32).reshape(FRAMES, TRACKS, CHANNELS)
    track_out = (tokens.astype(jnp.float32) + projected).astype(jnp.bfloat16)
    return refined_state, track_out
```

```python
import math

import jax
import jax.numpy as jnp
from jax import lax
from jax.experimental import pallas as pl
from jax.experimental.pallas import tpu as pltpu
from jax.sharding import PartitionSpec as P

HEADS = 8
HEAD_DIM = 32
GRU_WIDTH = 128
ITERS = 2
LOGIT_SCALE = HEAD_DIM ** (-0.5) * math.log2(math.e)
MASKED = -1e30
GROUP = 16
MESH = pl.DeviceIdType.MESH
F32 = jnp.float32
BF16 = jnp.bfloat16
N_IN = 15


def dot(a, b):
    return jnp.dot(a, b, preferred_element_type=F32)


def dot_nt(a, b):
    return lax.dot_general(a, b, (((1,), (1,)), ((), ())), preferred_element_type=F32)


def iota(shape, dim):
    return lax.broadcasted_iota(jnp.int32, shape, dim)


def softmax_rows(scores, bias):
    scores = scores * LOGIT_SCALE + bias
    top = jnp.max(scores, axis=-1, keepdims=True)
    powers = jnp.exp2(scores - top)
    total = jnp.sum(powers, axis=-1, keepdims=True)
    return (powers * (1.0 / total)).astype(BF16)


def column_taps(x, columns):
    length = x.shape[0]
    col = lax.rem(iota(x.shape, 0), columns)
    left = jnp.where(col == 0, 0.0, pltpu.roll(x, 1, 0))
    right = jnp.where(col == columns - 1, 0.0, pltpu.roll(x, length - 1, 0))
    return jnp.concatenate([left.astype(BF16), x.astype(BF16), right.astype(BF16)], axis=1)


def interior_conv(x, w_ref, low, columns):
    width = x.shape[1]
    taps = column_taps(x, columns)
    zero = jnp.zeros((columns, taps.shape[1]), BF16)
    above = jnp.concatenate([zero, taps[:-columns]], axis=0)
    below = jnp.concatenate([taps[columns:], zero], axis=0)
    patches = jnp.concatenate([above, taps, below], axis=1)
    weight = w_ref[:, :, low : low + width, :]
    return dot(patches, weight.reshape(9 * width, weight.shape[3]))


def kernel(frames, bands, *refs):
    inputs, refs = refs[:N_IN], refs[N_IN:]
    (out_state, out_track), refs = refs[:2], refs[2:]
    held, refs = refs[:N_IN], refs[N_IN:]
    (
        partner_tok,
        partner_vis,
        tok_all,
        vis_all,
        keys,
        values,
        t_q,
        t_k,
        t_v,
        att_out,
        returned,
        stages,
        halos,
        attended,
        acc_g,
        acc_c,
        ctx_g,
        ctx_c,
        in_sem,
        own_sem,
        partner_send,
        partner_recv,
        tok_send,
        tok_recv,
        vis_send,
        vis_recv,
        back_send,
        back_recv,
        halo_send,
        halo_recv,
    ) = refs
    (pix_h, gst_h, tok_h, vis_h) = inputs[:4]
    (pix, gst, tok, vis, qfr, wpq, wpk, wpv, wpo, wtq, wtk, wtv, wto, wg, wc) = held
    me = lax.axis_index("frame")
    band = lax.axis_index("band")
    other = lax.rem(band + 1, bands)
    tracks, channels = tok.shape[1], tok.shape[2]
    mine = tracks // frames
    rows, columns = pix.shape[1], pix.shape[2]
    pixels = rows * columns

    loads = [pltpu.make_async_copy(inputs[i], held[i], in_sem.at[i]) for i in range(N_IN)]
    for i in (2, 6, 7, 0, 5, 3, 4, 9, 10, 11, 8, 1, 13, 14, 12):
        loads[i].start()

    barrier = pltpu.get_barrier_semaphore()
    for k in range(1, frames):
        pl.semaphore_signal(
            barrier, inc=1, device_id={"frame": lax.rem(me + k, frames)}, device_id_type=MESH
        )
    pl.semaphore_signal(barrier, inc=1, device_id={"band": other}, device_id_type=MESH)
    pl.semaphore_wait(barrier, frames)

    def to_partner(src, dst, send, recv):
        return pltpu.make_async_remote_copy(
            src_ref=src,
            dst_ref=dst,
            send_sem=send,
            recv_sem=recv,
            device_id={"band": other},
            device_id_type=MESH,
        )

    def to_frame(k, src, dst, send, recv):
        return pltpu.make_async_remote_copy(
            src_ref=src,
            dst_ref=dst,
            send_sem=send.at[k],
            recv_sem=recv.at[k],
            device_id={"frame": lax.rem(me + k, frames)},
            device_id_type=MESH,
        )

    partner_copies = [
        to_partner(tok_h.at[0], partner_tok, partner_send.at[0], partner_recv.at[0]),
        to_partner(vis_h, partner_vis, partner_send.at[1], partner_recv.at[1]),
    ]
    edge_row = (1 - band) * (rows - 1)
    edge = pl.multiple_of(edge_row * columns, columns)
    halo_copies = [
        to_partner(gst_h.at[0, edge_row], halos.at[0], halo_send.at[0], halo_recv.at[0])
    ]
    for copy in partner_copies:
        copy.start()
    frame_copies = []
    for k in range(1, frames):
        target = lax.rem(me + k, frames)
        frame_copies.append(
            to_frame(
                k,
                tok_h.at[0, pl.ds(pl.multiple_of(target * mine, mine), mine)],
                tok_all.at[me],
                tok_send,
                tok_recv,
            )
        )
        frame_copies.append(to_frame(k, vis_h, vis_all.at[me], vis_send, vis_recv))
    for copy in frame_copies:
        copy.start()
    own_copies = [
        pltpu.make_async_copy(
            tok_h.at[0, pl.ds(pl.multiple_of(me * mine, mine), mine)],
            tok_all.at[me],
            own_sem.at[0],
        ),
        pltpu.make_async_copy(vis_h, vis_all.at[me], own_sem.at[1]),
    ]
    for copy in own_copies:
        copy.start()
    halo_copies[0].start()

    for i in (2, 6, 7):
        loads[i].wait()
    keys[0:tracks, :] = dot(tok[0], wpk[...]).astype(BF16)
    values[0:tracks, :] = dot(tok[0], wpv[...]).astype(BF16)
    for i in (0, 5, 3):
        loads[i].wait()
    queries = dot(pix[0].reshape(pixels, channels), wpq[...]).astype(BF16)
    for copy in partner_copies:
        copy.wait_recv()
    keys[tracks:, :] = dot(partner_tok[...], wpk[...]).astype(BF16)
    values[tracks:, :] = dot(partner_tok[...], wpv[...]).astype(BF16)
    seen = jnp.concatenate([vis[...], partner_vis[...]], axis=1)
    pixel_bias = jnp.where(seen > 0, 0.0, MASKED)
    lane_head = lax.div(iota((1, channels), 1), HEAD_DIM)
    attended[...] = jnp.zeros_like(attended)

    def pixel_head(h, carry):
        chosen = jnp.where(lane_head == h, 1.0, 0.0)
        weights = softmax_rows(dot_nt(queries * chosen.astype(BF16), keys[...]), pixel_bias)
        attended[...] += dot(weights, values[...]) * chosen
        return carry

    lax.fori_loop(0, HEADS, pixel_head, 0)
    loads[8].wait()
    context = dot(attended[...].astype(BF16), wpo[...]).astype(BF16)

    def share_edge(stage, value):
        stages[stage - 1, :, :] = value
        copy = to_partner(
            stages.at[stage - 1, pl.ds(edge, columns)],
            halos.at[stage],
            halo_send.at[stage],
            halo_recv.at[stage],
        )
        copy.start()
        halo_copies.append(copy)

    share_edge(1, context)

    for i in (4, 9, 10, 11):
        loads[i].wait()
    for copy in own_copies:
        copy.wait()
    for copy in frame_copies:
        copy.wait_recv()
    block = frames * GROUP
    flat = tok_all[...].reshape(frames * mine, channels)
    for weight, dst in ((wtq, t_q), (wtk, t_k), (wtv, t_v)):
        dst[...] = dot(flat, weight[...]).astype(BF16).reshape(frames, mine, channels)
    picked_shape = (tracks, frames * mine)
    slot = iota(picked_shape, 1)
    picked = me * mine + lax.div(slot, block) * GROUP + lax.rem(slot, GROUP)
    pick = jnp.where(iota(picked_shape, 0) == picked, 1.0, 0.0).astype(BF16)
    slot_frame = lax.rem(lax.div(iota((frames, frames * mine), 1), GROUP), frames)
    vis_rows = dot(vis_all[...].reshape(frames, tracks).astype(F32).astype(BF16), pick)
    vis_row = jnp.sum(
        jnp.where(slot_frame == iota(slot_frame.shape, 0), vis_rows, 0.0), axis=0, keepdims=True
    )
    query_rows = jnp.broadcast_to(qfr[...].astype(F32), (GROUP, tracks)).astype(BF16)
    query_row = dot(query_rows, pick)[0:1]
    same = lax.rem(iota((block, block), 0), GROUP) == lax.rem(iota((block, block), 1), GROUP)
    key_frame = lax.div(iota((block, block), 1), GROUP).astype(F32)
    together = max(1, min(HEADS, 1024 // block))
    for g in range(mine // GROUP):
        part = slice(g * GROUP, (g + 1) * GROUP)
        cols = slice(g * block, (g + 1) * block)
        q_g = t_q[:, part, :].reshape(block, channels)
        k_g = t_k[:, part, :].reshape(block, channels)
        v_g = t_v[:, part, :].reshape(block, channels)
        is_anchor = jnp.logical_and(same, key_frame == query_row[:, cols])
        anchor = dot(jnp.where(is_anchor, 1.0, 0.0).astype(BF16), q_g)
        joint = (q_g.astype(F32) + anchor).astype(BF16)
        allowed = jnp.logical_and(same, vis_row[:, cols] > 0.5)
        bias = jnp.where(allowed, 0.0, MASKED)
        biases = jnp.concatenate([bias] * together, axis=0)
        result = jnp.zeros((block, channels), F32)
        for first in range(0, HEADS, together):
            masks = [
                jnp.where(lane_head == first + h, 1.0, 0.0) for h in range(together)
            ]
            stacked = jnp.concatenate([joint * m.astype(BF16) for m in masks], axis=0)
            weights = softmax_rows(dot_nt(stacked, k_g), biases)
            mixed = dot(weights, v_g)
            for h in range(together):
                result = result + mixed[h * block : (h + 1) * block] * masks[h]
        att_out[:, part, :] = result.astype(BF16).reshape(frames, GROUP, channels)
    back_copies = []
    for k in range(1, frames):
        target = lax.rem(me + k, frames)
        back_copies.append(
            to_frame(k, att_out.at[target], returned.at[me], back_send, back_recv)
        )
    for copy in back_copies:
        copy.start()
    returned[pl.ds(me, 1)] = att_out[pl.ds(me, 1)]

    def add_halo(acc, stage, w_ref, low):
        taps = column_taps(halos[stage].astype(F32), columns)
        weight = w_ref[pl.ds((1 - band) * 2, 1), :, low : low + GRU_WIDTH, :]
        weight = weight.reshape(3 * GRU_WIDTH, weight.shape[3])
        acc[pl.ds(edge, columns), :] += dot(taps, weight)

    for i in (1, 13, 14):
        loads[i].wait()
    context_f32 = context.astype(F32)
    ctx_g[...] = interior_conv(context_f32, wg, GRU_WIDTH, columns)
    ctx_c[...] = interior_conv(context_f32, wc, GRU_WIDTH, columns)
    halo_copies[1].wait_recv()
    add_halo(ctx_g, 1, wg, GRU_WIDTH)
    add_halo(ctx_c, 1, wc, GRU_WIDTH)
    state = gst[0].reshape(pixels, GRU_WIDTH).astype(F32)
    state_stage = 0
    for iteration in range(ITERS):
        acc_g[...] = ctx_g[...] + interior_conv(state, wg, 0, columns)
        halo_copies[state_stage].wait_recv()
        add_halo(acc_g, state_stage, wg, 0)
        reset = jax.nn.sigmoid(acc_g[:, GRU_WIDTH:])
        reset_state = (reset * state).astype(BF16)
        share_edge(2 + 2 * iteration, reset_state)
        update = jax.nn.sigmoid(acc_g[:, :GRU_WIDTH])
        acc_c[...] = ctx_c[...] + interior_conv(reset_state.astype(F32), wc, 0, columns)
        halo_copies[2 + 2 * iteration].wait_recv()
        add_halo(acc_c, 2 + 2 * iteration, wc, 0)
        candidate = jnp.tanh(acc_c[...])
        new_state = ((1.0 - update) * state + update * candidate).astype(BF16)
        if iteration < ITERS - 1:
            state_stage = 3 + 2 * iteration
            share_edge(state_stage, new_state)
            state = new_state.astype(F32)
    out_state[...] = new_state.reshape(1, rows, columns, GRU_WIDTH)

    loads[12].wait()
    for copy in back_copies:
        copy.wait_recv()
    track_update = dot(returned[...].reshape(tracks, channels), wto[...])
    out_track[0] = (tok[0].astype(F32) + track_update).astype(BF16)
    for copy in partner_copies + frame_copies + back_copies + halo_copies:
        copy.wait_send()


def on_device(frames, bands, *args):
    args = list(args)
    args[4] = args[4].reshape(1, -1)
    pixels, gru_state, tokens, visible = args[:4]
    tracks, channels = tokens.shape[1:]
    mine = tracks // frames
    rows, columns = pixels.shape[1:3]
    count = rows * columns
    halo_stages = 1 + 2 * ITERS
    dma = pltpu.SemaphoreType.DMA
    scratch = [pltpu.VMEM(a.shape, a.dtype) for a in args] + [
        pltpu.VMEM((tracks, channels), BF16),
        pltpu.VMEM((1, tracks), jnp.int32),
        pltpu.VMEM((frames, mine, channels), BF16),
        pltpu.VMEM((frames, 1, tracks), jnp.int32),
        pltpu.VMEM((2 * tracks, channels), BF16),
        pltpu.VMEM((2 * tracks, channels), BF16),
        pltpu.VMEM((frames, mine, channels), BF16),
        pltpu.VMEM((frames, mine, channels), BF16),
        pltpu.VMEM((frames, mine, channels), BF16),
        pltpu.VMEM((frames, mine, channels), BF16),
        pltpu.VMEM((frames, mine, channels), BF16),
        pltpu.VMEM((halo_stages - 1, count, GRU_WIDTH), BF16),
        pltpu.VMEM((halo_stages, columns, GRU_WIDTH), BF16),
        pltpu.VMEM((count, channels), F32),
        pltpu.VMEM((count, 2 * GRU_WIDTH), F32),
        pltpu.VMEM((count, GRU_WIDTH), F32),
        pltpu.VMEM((count, 2 * GRU_WIDTH), F32),
        pltpu.VMEM((count, GRU_WIDTH), F32),
        dma((N_IN,)),
        dma((2,)),
        dma((2,)),
        dma((2,)),
        dma((frames,)),
        dma((frames,)),
        dma((frames,)),
        dma((frames,)),
        dma((frames,)),
        dma((frames,)),
        dma((halo_stages,)),
        dma((halo_stages,)),
    ]

    def body(*refs):
        kernel(frames, bands, *refs)

    return pl.pallas_call(
        body,
        out_shape=(
            jax.ShapeDtypeStruct(gru_state.shape, BF16),
            jax.ShapeDtypeStruct(tokens.shape, BF16),
        ),
        in_specs=[pl.BlockSpec(memory_space=pl.ANY)] * N_IN,
        out_specs=(pl.BlockSpec(memory_space=pltpu.VMEM),) * 2,
        scratch_shapes=scratch,
        compiler_params=pltpu.CompilerParams(collective_id=0, has_side_effects=True),
        name="track_step",
    )(*args)


def solution(mesh):
    frames, bands = mesh.shape["frame"], mesh.shape["band"]
    placed = (
        P(("clip", "frame"), "band", None, None),
        P(("clip", "frame"), "band", None, None),
        P(("clip", "frame"), "band", None),
        P(("clip", "frame"), "band"),
        P(("clip", "band")),
    ) + (P(),) * 10
    return jax.shard_map(
        lambda *args: on_device(frames, bands, *args),
        mesh=mesh,
        in_specs=placed,
        out_specs=(P(("clip", "frame"), "band", None, None), P(("clip", "frame"), "band", None)),
        check_vma=False,
    )
```

```python
import math

import jax
import jax.numpy as jnp
from jax import lax
from jax.experimental import pallas as pl
from jax.experimental.pallas import tpu as pltpu
from jax.sharding import PartitionSpec as P

HEADS = 8
HEAD_DIM = 32
GRU_WIDTH = 128
ITERS = 2
LOGIT_SCALE = HEAD_DIM ** (-0.5) * math.log2(math.e)
MASKED = -1e30
GROUP = 16
MESH = pl.DeviceIdType.MESH
F32 = jnp.float32
BF16 = jnp.bfloat16
N_IN = 14
UNROLL = 4


def dot(a, b):
    return jnp.dot(a, b, preferred_element_type=F32)


def dot_nt(a, b):
    return lax.dot_general(a, b, (((1,), (1,)), ((), ())), preferred_element_type=F32)


def iota(shape, dim):
    return lax.broadcasted_iota(jnp.int32, shape, dim)


def softmax_rows(scores, bias):
    scores = scores * LOGIT_SCALE + bias
    top = jnp.max(scores, axis=-1, keepdims=True)
    powers = jnp.exp2(scores - top)
    total = jnp.sum(powers, axis=-1, keepdims=True)
    return (powers * (1.0 / total)).astype(BF16)


def column_taps(x, columns):
    length = x.shape[0]
    col = lax.rem(iota(x.shape, 0), columns)
    left = jnp.where(col == 0, 0.0, pltpu.roll(x, 1, 0))
    right = jnp.where(col == columns - 1, 0.0, pltpu.roll(x, length - 1, 0))
    return jnp.concatenate([left.astype(BF16), x.astype(BF16), right.astype(BF16)], axis=1)


def interior_conv(x, w_ref, low, columns):
    width = x.shape[1]
    taps = column_taps(x, columns)
    zero = jnp.zeros((columns, taps.shape[1]), BF16)
    above = jnp.concatenate([zero, taps[:-columns]], axis=0)
    below = jnp.concatenate([taps[columns:], zero], axis=0)
    patches = jnp.concatenate([above, taps, below], axis=1)
    weight = w_ref[:, :, low : low + width, :]
    return dot(patches, weight.reshape(9 * width, weight.shape[3]))


def kernel(frames, bands, *refs):
    inputs, refs = refs[:N_IN], refs[N_IN:]
    (out_state, returned), refs = refs[:2], refs[2:]
    held, refs = refs[:N_IN], refs[N_IN:]
    (
        partner_tok,
        partner_vis,
        tok_all,
        vis_all,
        queries,
        keys,
        values,
        att_out,
        stages,
        halos,
        attended,
        tops,
        totals,
        acc_g,
        acc_c,
        ctx_g,
        ctx_c,
        in_sem,
        own_sem,
        partner_send,
        partner_recv,
        tok_send,
        tok_recv,
        vis_send,
        vis_recv,
        back_send,
        back_recv,
        back_own,
        halo_send,
        halo_recv,
    ) = refs
    (pix_h, gst_h, tok_h, vis_h) = inputs[:4]
    (pix, gst, tok, vis, qfr, wpq, wpk, wpv, wpo, wtq, wtk, wtv, wg, wc) = held
    me = lax.axis_index("frame")
    band = lax.axis_index("band")
    other = lax.rem(band + 1, bands)
    tracks, channels = tok.shape[1], tok.shape[2]
    mine = tracks // frames
    chunks, part_rows = tok_all.shape[0], tok_all.shape[2]
    rows, columns = pix.shape[1], pix.shape[2]
    pixels = rows * columns

    loads = [pltpu.make_async_copy(inputs[i], held[i], in_sem.at[i]) for i in range(N_IN)]
    for i in (2, 6, 7, 0, 5, 3, 8, 4, 9, 10, 11, 1, 12, 13):
        loads[i].start()

    barrier = pltpu.get_barrier_semaphore()
    for k in range(1, frames):
        pl.semaphore_signal(
            barrier, inc=1, device_id={"frame": lax.rem(me + k, frames)}, device_id_type=MESH
        )
    pl.semaphore_signal(barrier, inc=1, device_id={"band": other}, device_id_type=MESH)

    for i in (2, 6, 7):
        loads[i].wait()
    lane_head = lax.div(iota((1, channels), 1), HEAD_DIM)
    attended[...] = jnp.zeros_like(attended)
    tops[...] = jnp.zeros_like(tops)
    totals[...] = jnp.zeros_like(totals)

    def attend_half(half, track_rows, seen):
        keys[...] = dot(track_rows, wpk[...]).astype(BF16)
        values[...] = dot(track_rows, wpv[...]).astype(BF16)
        bias = jnp.where(seen > 0, 0.0, MASKED)

        def pixel_head(h, carry):
            chosen = jnp.where(lane_head == h, 1.0, 0.0)
            scores = dot_nt(queries[...] * chosen.astype(BF16), keys[...])
            scores = scores * LOGIT_SCALE + bias
            top = jnp.max(scores, axis=-1, keepdims=True)
            powers = jnp.exp2(scores - top)
            total = jnp.sum(powers, axis=-1, keepdims=True)
            tops[half] += top * chosen
            totals[half] += total * chosen
            attended[half] += dot(powers.astype(BF16), values[...]) * chosen
            return carry

        lax.fori_loop(0, HEADS, pixel_head, 0, unroll=UNROLL)

    for i in (0, 5, 3):
        loads[i].wait()
    queries[...] = dot(pix[0].reshape(pixels, channels), wpq[...]).astype(BF16)
    attend_half(0, tok[0], vis[...])
    pl.semaphore_wait(barrier, frames)

    def to_partner(src, dst, send, recv):
        return pltpu.make_async_remote_copy(
            src_ref=src,
            dst_ref=dst,
            send_sem=send,
            recv_sem=recv,
            device_id={"band": other},
            device_id_type=MESH,
        )

    def to_frame(k, src, dst, send, recv):
        return pltpu.make_async_remote_copy(
            src_ref=src,
            dst_ref=dst,
            send_sem=send,
            recv_sem=recv,
            device_id={"frame": lax.rem(me + k, frames)},
            device_id_type=MESH,
        )

    partner_copies = [
        to_partner(tok_h.at[0], partner_tok, partner_send.at[0], partner_recv.at[0]),
        to_partner(vis_h, partner_vis, partner_send.at[1], partner_recv.at[1]),
    ]
    edge_row = (1 - band) * (rows - 1)
    edge = pl.multiple_of(edge_row * columns, columns)
    halo_copies = [
        to_partner(gst_h.at[0, edge_row], halos.at[0], halo_send.at[0], halo_recv.at[0])
    ]
    for copy in partner_copies:
        copy.start()
    order = sorted(range(1, frames), key=lambda k: -min(k, frames - k))
    vis_copies = [
        to_frame(k, vis_h, vis_all.at[me], vis_send.at[k], vis_recv.at[k]) for k in order
    ]
    tok_copies = []
    for c in range(chunks):
        for k in order:
            target = lax.rem(me + k, frames)
            start = pl.multiple_of(target * mine + c * part_rows, part_rows)
            tok_copies.append(
                to_frame(
                    k,
                    tok_h.at[0, pl.ds(start, part_rows)],
                    tok_all.at[c, me],
                    tok_send.at[c, k],
                    tok_recv.at[c, k],
                )
            )
    for copy in vis_copies + tok_copies:
        copy.start()
    own_copies = [
        pltpu.make_async_copy(
            tok_h.at[0, pl.ds(pl.multiple_of(me * mine + c * part_rows, part_rows), part_rows)],
            tok_all.at[c, me],
            own_sem.at[c],
        )
        for c in range(chunks)
    ]
    own_copies.append(pltpu.make_async_copy(vis_h, vis_all.at[me], own_sem.at[chunks]))
    for copy in own_copies:
        copy.start()
    halo_copies[0].start()

    for copy in partner_copies:
        copy.wait_recv()
    attend_half(1, partner_tok[...], partner_vis[...])
    highest = jnp.maximum(tops[0], tops[1])
    share_0 = jnp.exp2(tops[0] - highest)
    share_1 = jnp.exp2(tops[1] - highest)
    merged = (attended[0] * share_0 + attended[1] * share_1) / (
        totals[0] * share_0 + totals[1] * share_1
    )
    loads[8].wait()
    context = dot(merged.astype(BF16), wpo[...]).astype(BF16)

    def share_edge(stage, value):
        stages[stage - 1, :, :] = value
        copy = to_partner(
            stages.at[stage - 1, pl.ds(edge, columns)],
            halos.at[stage],
            halo_send.at[stage],
            halo_recv.at[stage],
        )
        copy.start()
        halo_copies.append(copy)

    share_edge(1, context)

    for i in (4, 9, 10, 11):
        loads[i].wait()
    for copy in own_copies:
        copy.wait()
    for copy in vis_copies:
        copy.wait_recv()
    block = frames * GROUP
    picked_shape = (tracks, frames * mine)
    slot = iota(picked_shape, 1)
    picked = me * mine + lax.div(slot, block) * GROUP + lax.rem(slot, GROUP)
    pick = jnp.where(iota(picked_shape, 0) == picked, 1.0, 0.0).astype(BF16)
    slot_frame = lax.rem(lax.div(iota((frames, frames * mine), 1), GROUP), frames)
    vis_rows = dot(vis_all[...].reshape(frames, tracks).astype(F32).astype(BF16), pick)
    vis_row = jnp.sum(
        jnp.where(slot_frame == iota(slot_frame.shape, 0), vis_rows, 0.0), axis=0, keepdims=True
    )
    query_rows = jnp.broadcast_to(qfr[...].astype(F32), (GROUP, tracks)).astype(BF16)
    query_row = dot(query_rows, pick)[0:1]
    same = lax.rem(iota((block, block), 0), GROUP) == lax.rem(iota((block, block), 1), GROUP)
    key_frame = lax.div(iota((block, block), 1), GROUP).astype(F32)
    together = max(1, min(HEADS, 1024 // block))
    back_copies = []
    own_back = []

    def attend_time(c):
        for copy in tok_copies[c * (frames - 1) : (c + 1) * (frames - 1)]:
            copy.wait_recv()
        flat = tok_all[c].reshape(frames * part_rows, channels)
        t_q, t_k, t_v = [
            dot(flat, weight[...]).astype(BF16).reshape(frames, part_rows, channels)
            for weight in (wtq, wtk, wtv)
        ]
        for g in range(part_rows // GROUP):
            part = slice(g * GROUP, (g + 1) * GROUP)
            first_col = (c * (part_rows // GROUP) + g) * block
            cols = slice(first_col, first_col + block)
            q_g = t_q[:, part, :].reshape(block, channels)
            k_g = t_k[:, part, :].reshape(block, channels)
            v_g = t_v[:, part, :].reshape(block, channels)
            is_anchor = jnp.logical_and(same, key_frame == query_row[:, cols])
            anchor = dot(jnp.where(is_anchor, 1.0, 0.0).astype(BF16), q_g)
            joint = (q_g.astype(F32) + anchor).astype(BF16)
            allowed = jnp.logical_and(same, vis_row[:, cols] > 0.5)
            bias = jnp.where(allowed, 0.0, MASKED)
            biases = jnp.concatenate([bias] * together, axis=0)
            result = jnp.zeros((block, channels), F32)
            for first in range(0, HEADS, together):
                masks = [jnp.where(lane_head == first + h, 1.0, 0.0) for h in range(together)]
                stacked = jnp.concatenate([joint * m.astype(BF16) for m in masks], axis=0)
                weights = softmax_rows(dot_nt(stacked, k_g), biases)
                mixed = dot(weights, v_g)
                for h in range(together):
                    result = result + mixed[h * block : (h + 1) * block] * masks[h]
            att_out[c, :, part, :] = result.astype(BF16).reshape(frames, GROUP, channels)
        there = pl.ds(c * part_rows, part_rows)
        for k in order:
            target = lax.rem(me + k, frames)
            copy = to_frame(
                k,
                att_out.at[c, target],
                returned.at[me, there],
                back_send.at[c, k],
                back_recv.at[c, k],
            )
            copy.start()
            back_copies.append(copy)
        copy = pltpu.make_async_copy(att_out.at[c, me], returned.at[me, there], back_own.at[c])
        copy.start()
        own_back.append(copy)

    attend_time(0)

    def add_halo(acc, stage, w_ref, low):
        taps = column_taps(halos[stage].astype(F32), columns)
        weight = w_ref[pl.ds((1 - band) * 2, 1), :, low : low + GRU_WIDTH, :]
        weight = weight.reshape(3 * GRU_WIDTH, weight.shape[3])
        acc[pl.ds(edge, columns), :] += dot(taps, weight)

    for i in (1, 12, 13):
        loads[i].wait()
    context_f32 = context.astype(F32)
    ctx_g[...] = interior_conv(context_f32, wg, GRU_WIDTH, columns)
    ctx_c[...] = interior_conv(context_f32, wc, GRU_WIDTH, columns)
    halo_copies[1].wait_recv()
    add_halo(ctx_g, 1, wg, GRU_WIDTH)
    add_halo(ctx_c, 1, wc, GRU_WIDTH)
    for c in range(1, chunks):
        attend_time(c)
    state = gst[0].reshape(pixels, GRU_WIDTH).astype(F32)
    state_stage = 0
    for iteration in range(ITERS):
        acc_g[...] = ctx_g[...] + interior_conv(state, wg, 0, columns)
        halo_copies[state_stage].wait_recv()
        add_halo(acc_g, state_stage, wg, 0)
        reset = jax.nn.sigmoid(acc_g[:, GRU_WIDTH:])
        reset_state = (reset * state).astype(BF16)
        share_edge(2 + 2 * iteration, reset_state)
        update = jax.nn.sigmoid(acc_g[:, :GRU_WIDTH])
        acc_c[...] = ctx_c[...] + interior_conv(reset_state.astype(F32), wc, 0, columns)
        halo_copies[2 + 2 * iteration].wait_recv()
        add_halo(acc_c, 2 + 2 * iteration, wc, 0)
        candidate = jnp.tanh(acc_c[...])
        new_state = ((1.0 - update) * state + update * candidate).astype(BF16)
        if iteration < ITERS - 1:
            state_stage = 3 + 2 * iteration
            share_edge(state_stage, new_state)
            state = new_state.astype(F32)
    out_state[...] = new_state.reshape(1, rows, columns, GRU_WIDTH)

    for copy in own_back:
        copy.wait()
    for copy in back_copies:
        copy.wait_recv()
    for copy in partner_copies + vis_copies + tok_copies + back_copies + halo_copies:
        copy.wait_send()


def finish(state, tok, returned, wto, out_state, out_track):
    out_state[...] = state[...]
    update = dot(returned[...].reshape(tok.shape[1], tok.shape[2]), wto[...])
    out_track[0] = (tok[0].astype(F32) + update).astype(BF16)


def on_device(frames, bands, *args):
    args = list(args)
    args[4] = args[4].reshape(1, -1)
    time_out = args.pop(12)
    pixels, gru_state, tokens, visible = args[:4]
    tracks, channels = tokens.shape[1:]
    mine = tracks // frames
    chunks = 2 if mine % (2 * GROUP) == 0 else 1
    part_rows = mine // chunks
    rows, columns = pixels.shape[1:3]
    count = rows * columns
    halo_stages = 1 + 2 * ITERS
    dma = pltpu.SemaphoreType.DMA
    scratch = [pltpu.VMEM(a.shape, a.dtype) for a in args] + [
        pltpu.VMEM((tracks, channels), BF16),
        pltpu.VMEM((1, tracks), jnp.int32),
        pltpu.VMEM((chunks, frames, part_rows, channels), BF16),
        pltpu.VMEM((frames, 1, tracks), jnp.int32),
        pltpu.VMEM((count, channels), BF16),
        pltpu.VMEM((tracks, channels), BF16),
        pltpu.VMEM((tracks, channels), BF16),
        pltpu.VMEM((chunks, frames, part_rows, channels), BF16),
        pltpu.VMEM((halo_stages - 1, count, GRU_WIDTH), BF16),
        pltpu.VMEM((halo_stages, columns, GRU_WIDTH), BF16),
        pltpu.VMEM((2, count, channels), F32),
        pltpu.VMEM((2, count, channels), F32),
        pltpu.VMEM((2, count, channels), F32),
        pltpu.VMEM((count, 2 * GRU_WIDTH), F32),
        pltpu.VMEM((count, GRU_WIDTH), F32),
        pltpu.VMEM((count, 2 * GRU_WIDTH), F32),
        pltpu.VMEM((count, GRU_WIDTH), F32),
        dma((N_IN,)),
        dma((chunks + 1,)),
        dma((2,)),
        dma((2,)),
        dma((chunks, frames)),
        dma((chunks, frames)),
        dma((frames,)),
        dma((frames,)),
        dma((chunks, frames)),
        dma((chunks, frames)),
        dma((chunks,)),
        dma((halo_stages,)),
        dma((halo_stages,)),
    ]

    def body(*refs):
        kernel(frames, bands, *refs)

    state, returned = pl.pallas_call(
        body,
        out_shape=(
            jax.ShapeDtypeStruct(gru_state.shape, BF16),
            jax.ShapeDtypeStruct((frames, mine, channels), BF16),
        ),
        in_specs=[pl.BlockSpec(memory_space=pl.ANY)] * N_IN,
        out_specs=(
            pl.BlockSpec(memory_space=pltpu.VMEM),
            pl.BlockSpec(memory_space=pl.ANY),
        ),
        scratch_shapes=scratch,
        compiler_params=pltpu.CompilerParams(collective_id=0, has_side_effects=True),
        name="track_step",
    )(*args)
    return pl.pallas_call(
        finish,
        out_shape=(
            jax.ShapeDtypeStruct(gru_state.shape, BF16),
            jax.ShapeDtypeStruct(tokens.shape, BF16),
        ),
        in_specs=[pl.BlockSpec(memory_space=pltpu.VMEM)] * 4,
        out_specs=(pl.BlockSpec(memory_space=pltpu.VMEM),) * 2,
        name="track_finish",
    )(state, tokens, returned, time_out)


def solution(mesh):
    frames, bands = mesh.shape["frame"], mesh.shape["band"]
    placed = (
        P(("clip", "frame"), "band", None, None),
        P(("clip", "frame"), "band", None, None),
        P(("clip", "frame"), "band", None),
        P(("clip", "frame"), "band"),
        P(("clip", "band")),
    ) + (P(),) * 10
    return jax.shard_map(
        lambda *args: on_device(frames, bands, *args),
        mesh=mesh,
        in_specs=placed,
        out_specs=(P(("clip", "frame"), "band", None, None), P(("clip", "frame"), "band", None)),
        check_vma=False,
    )
```

```python
import math

import jax
import jax.numpy as jnp
from jax import lax
from jax.experimental import pallas as pl
from jax.experimental.pallas import tpu as pltpu
from jax.sharding import PartitionSpec as P

HEADS = 8
HEAD_DIM = 32
GRU_WIDTH = 128
ITERS = 2
LOGIT_SCALE = HEAD_DIM ** (-0.5) * math.log2(math.e)
MASKED = -1e30
GROUP = 16
MESH = pl.DeviceIdType.MESH
F32 = jnp.float32
BF16 = jnp.bfloat16
N_IN = 14
UNROLL = 4
BEFORE = 4


def dot(a, b):
    return jnp.dot(a, b, preferred_element_type=F32)


def dot_nt(a, b):
    return lax.dot_general(a, b, (((1,), (1,)), ((), ())), preferred_element_type=F32)


def iota(shape, dim):
    return lax.broadcasted_iota(jnp.int32, shape, dim)


def softmax_rows(scores, bias):
    scores = scores * LOGIT_SCALE + bias
    top = jnp.max(scores, axis=-1, keepdims=True)
    powers = jnp.exp2(scores - top)
    total = jnp.sum(powers, axis=-1, keepdims=True)
    return (powers * (1.0 / total)).astype(BF16)


def column_taps(x, columns):
    length = x.shape[0]
    col = lax.rem(iota(x.shape, 0), columns)
    left = jnp.where(col == 0, 0.0, pltpu.roll(x, 1, 0))
    right = jnp.where(col == columns - 1, 0.0, pltpu.roll(x, length - 1, 0))
    return jnp.concatenate([left.astype(BF16), x.astype(BF16), right.astype(BF16)], axis=1)


def interior_conv(x, w_ref, low, columns):
    width = x.shape[1]
    taps = column_taps(x, columns)
    zero = jnp.zeros((columns, taps.shape[1]), BF16)
    above = jnp.concatenate([zero, taps[:-columns]], axis=0)
    below = jnp.concatenate([taps[columns:], zero], axis=0)
    patches = jnp.concatenate([above, taps, below], axis=1)
    weight = w_ref[:, :, low : low + width, :]
    return dot(patches, weight.reshape(9 * width, weight.shape[3]))


def kernel(frames, bands, *refs):
    inputs, refs = refs[:N_IN], refs[N_IN:]
    (out_state, returned), refs = refs[:2], refs[2:]
    held, refs = refs[:N_IN], refs[N_IN:]
    (
        partner_tok,
        partner_vis,
        tok_all,
        vis_all,
        queries,
        keys,
        values,
        att_out,
        stages,
        halos,
        attended,
        tops,
        totals,
        acc_g,
        acc_c,
        ctx_g,
        ctx_c,
        in_sem,
        own_sem,
        partner_send,
        partner_recv,
        tok_send,
        tok_recv,
        vis_send,
        vis_recv,
        back_send,
        back_recv,
        back_own,
        halo_send,
        halo_recv,
    ) = refs
    (pix_h, gst_h, tok_h, vis_h) = inputs[:4]
    (pix, gst, tok, vis, qfr, wpq, wpk, wpv, wpo, wtq, wtk, wtv, wg, wc) = held
    me = lax.axis_index("frame")
    band = lax.axis_index("band")
    other = lax.rem(band + 1, bands)
    tracks, channels = tok.shape[1], tok.shape[2]
    mine = tracks // frames
    chunks, part_rows = tok_all.shape[0], tok_all.shape[2]
    rows, columns = pix.shape[1], pix.shape[2]
    pixels = rows * columns

    loads = [pltpu.make_async_copy(inputs[i], held[i], in_sem.at[i]) for i in range(N_IN)]
    for i in (2, 6, 7, 0, 5, 3, 8, 4, 9, 10, 11, 1, 12, 13):
        loads[i].start()

    barrier = pltpu.get_barrier_semaphore()
    for k in range(1, frames):
        pl.semaphore_signal(
            barrier, inc=1, device_id={"frame": lax.rem(me + k, frames)}, device_id_type=MESH
        )
    pl.semaphore_signal(barrier, inc=1, device_id={"band": other}, device_id_type=MESH)

    for i in (2, 6, 7):
        loads[i].wait()
    lane_head = lax.div(iota((1, channels), 1), HEAD_DIM)
    attended[...] = jnp.zeros_like(attended)
    tops[...] = jnp.zeros_like(tops)
    totals[...] = jnp.zeros_like(totals)

    def attend_half(half, track_rows, seen, middle=None):
        keys[...] = dot(track_rows, wpk[...]).astype(BF16)
        values[...] = dot(track_rows, wpv[...]).astype(BF16)
        bias = jnp.where(seen > 0, 0.0, MASKED)

        def pixel_head(h, carry):
            chosen = jnp.where(lane_head == h, 1.0, 0.0)
            scores = dot_nt(queries[...] * chosen.astype(BF16), keys[...])
            scores = scores * LOGIT_SCALE + bias
            top = jnp.max(scores, axis=-1, keepdims=True)
            powers = jnp.exp2(scores - top)
            total = jnp.sum(powers, axis=-1, keepdims=True)
            tops[half] += top * chosen
            totals[half] += total * chosen
            attended[half] += dot(powers.astype(BF16), values[...]) * chosen
            return carry

        if middle is None:
            lax.fori_loop(0, HEADS, pixel_head, 0, unroll=UNROLL)
        else:
            lax.fori_loop(0, BEFORE, pixel_head, 0, unroll=UNROLL)
            middle()
            lax.fori_loop(BEFORE, HEADS, pixel_head, 0, unroll=UNROLL)

    for i in (0, 5, 3):
        loads[i].wait()
    queries[...] = dot(pix[0].reshape(pixels, channels), wpq[...]).astype(BF16)

    def to_partner(src, dst, send, recv):
        return pltpu.make_async_remote_copy(
            src_ref=src,
            dst_ref=dst,
            send_sem=send,
            recv_sem=recv,
            device_id={"band": other},
            device_id_type=MESH,
        )

    def to_frame(k, src, dst, send, recv):
        return pltpu.make_async_remote_copy(
            src_ref=src,
            dst_ref=dst,
            send_sem=send,
            recv_sem=recv,
            device_id={"frame": lax.rem(me + k, frames)},
            device_id_type=MESH,
        )

    partner_copies = [
        to_partner(tok_h.at[0], partner_tok, partner_send.at[0], partner_recv.at[0]),
        to_partner(vis_h, partner_vis, partner_send.at[1], partner_recv.at[1]),
    ]
    edge_row = (1 - band) * (rows - 1)
    edge = pl.multiple_of(edge_row * columns, columns)
    halo_copies = [
        to_partner(gst_h.at[0, edge_row], halos.at[0], halo_send.at[0], halo_recv.at[0])
    ]
    order = sorted(range(1, frames), key=lambda k: -min(k, frames - k))
    vis_copies = [
        to_frame(k, vis_h, vis_all.at[me], vis_send.at[k], vis_recv.at[k]) for k in order
    ]
    tok_copies = []
    for c in range(chunks):
        for k in order:
            target = lax.rem(me + k, frames)
            start = pl.multiple_of(target * mine + c * part_rows, part_rows)
            tok_copies.append(
                to_frame(
                    k,
                    tok_h.at[0, pl.ds(start, part_rows)],
                    tok_all.at[c, me],
                    tok_send.at[c, k],
                    tok_recv.at[c, k],
                )
            )
    own_copies = [
        pltpu.make_async_copy(
            tok_h.at[0, pl.ds(pl.multiple_of(me * mine + c * part_rows, part_rows), part_rows)],
            tok_all.at[c, me],
            own_sem.at[c],
        )
        for c in range(chunks)
    ]
    own_copies.append(pltpu.make_async_copy(vis_h, vis_all.at[me], own_sem.at[chunks]))


    def start_sends():
        pl.semaphore_wait(barrier, frames)
        for copy in partner_copies:
            copy.start()
        for copy in vis_copies + tok_copies:
            copy.start()
        for copy in own_copies:
            copy.start()
        halo_copies[0].start()

    attend_half(0, tok[0], vis[...], start_sends)
    for copy in partner_copies:
        copy.wait_recv()
    attend_half(1, partner_tok[...], partner_vis[...])
    highest = jnp.maximum(tops[0], tops[1])
    share_0 = jnp.exp2(tops[0] - highest)
    share_1 = jnp.exp2(tops[1] - highest)
    merged = (attended[0] * share_0 + attended[1] * share_1) / (
        totals[0] * share_0 + totals[1] * share_1
    )
    loads[8].wait()
    context = dot(merged.astype(BF16), wpo[...]).astype(BF16)

    def share_edge(stage, value):
        stages[stage - 1, :, :] = value
        copy = to_partner(
            stages.at[stage - 1, pl.ds(edge, columns)],
            halos.at[stage],
            halo_send.at[stage],
            halo_recv.at[stage],
        )
        copy.start()
        halo_copies.append(copy)

    share_edge(1, context)

    for i in (4, 9, 10, 11):
        loads[i].wait()
    for copy in own_copies:
        copy.wait()
    for copy in vis_copies:
        copy.wait_recv()
    block = frames * GROUP
    picked_shape = (tracks, frames * mine)
    slot = iota(picked_shape, 1)
    picked = me * mine + lax.div(slot, block) * GROUP + lax.rem(slot, GROUP)
    pick = jnp.where(iota(picked_shape, 0) == picked, 1.0, 0.0).astype(BF16)
    slot_frame = lax.rem(lax.div(iota((frames, frames * mine), 1), GROUP), frames)
    vis_rows = dot(vis_all[...].reshape(frames, tracks).astype(F32).astype(BF16), pick)
    vis_row = jnp.sum(
        jnp.where(slot_frame == iota(slot_frame.shape, 0), vis_rows, 0.0), axis=0, keepdims=True
    )
    query_rows = jnp.broadcast_to(qfr[...].astype(F32), (GROUP, tracks)).astype(BF16)
    query_row = dot(query_rows, pick)[0:1]
    same = lax.rem(iota((block, block), 0), GROUP) == lax.rem(iota((block, block), 1), GROUP)
    key_frame = lax.div(iota((block, block), 1), GROUP).astype(F32)
    together = max(1, min(HEADS, 1024 // block))
    back_copies = []
    own_back = []

    def attend_time(c):
        for copy in tok_copies[c * (frames - 1) : (c + 1) * (frames - 1)]:
            copy.wait_recv()
        flat = tok_all[c].reshape(frames * part_rows, channels)
        t_q, t_k, t_v = [
            dot(flat, weight[...]).astype(BF16).reshape(frames, part_rows, channels)
            for weight in (wtq, wtk, wtv)
        ]
        for g in range(part_rows // GROUP):
            part = slice(g * GROUP, (g + 1) * GROUP)
            first_col = (c * (part_rows // GROUP) + g) * block
            cols = slice(first_col, first_col + block)
            q_g = t_q[:, part, :].reshape(block, channels)
            k_g = t_k[:, part, :].reshape(block, channels)
            v_g = t_v[:, part, :].reshape(block, channels)
            is_anchor = jnp.logical_and(same, key_frame == query_row[:, cols])
            anchor = dot(jnp.where(is_anchor, 1.0, 0.0).astype(BF16), q_g)
            joint = (q_g.astype(F32) + anchor).astype(BF16)
            allowed = jnp.logical_and(same, vis_row[:, cols] > 0.5)
            bias = jnp.where(allowed, 0.0, MASKED)
            biases = jnp.concatenate([bias] * together, axis=0)
            result = jnp.zeros((block, channels), F32)
            for first in range(0, HEADS, together):
                masks = [jnp.where(lane_head == first + h, 1.0, 0.0) for h in range(together)]
                stacked = jnp.concatenate([joint * m.astype(BF16) for m in masks], axis=0)
                weights = softmax_rows(dot_nt(stacked, k_g), biases)
                mixed = dot(weights, v_g)
                for h in range(together):
                    result = result + mixed[h * block : (h + 1) * block] * masks[h]
            att_out[c, :, part, :] = result.astype(BF16).reshape(frames, GROUP, channels)
        there = pl.ds(c * part_rows, part_rows)
        for k in order:
            target = lax.rem(me + k, frames)
            copy = to_frame(
                k,
                att_out.at[c, target],
                returned.at[me, there],
                back_send.at[c, k],
                back_recv.at[c, k],
            )
            copy.start()
            back_copies.append(copy)
        copy = pltpu.make_async_copy(att_out.at[c, me], returned.at[me, there], back_own.at[c])
        copy.start()
        own_back.append(copy)

    for c in range(chunks):
        attend_time(c)

    def add_halo(acc, stage, w_ref, low):
        taps = column_taps(halos[stage].astype(F32), columns)
        weight = w_ref[pl.ds((1 - band) * 2, 1), :, low : low + GRU_WIDTH, :]
        weight = weight.reshape(3 * GRU_WIDTH, weight.shape[3])
        acc[pl.ds(edge, columns), :] += dot(taps, weight)

    for i in (1, 12, 13):
        loads[i].wait()
    context_f32 = context.astype(F32)
    ctx_g[...] = interior_conv(context_f32, wg, GRU_WIDTH, columns)
    ctx_c[...] = interior_conv(context_f32, wc, GRU_WIDTH, columns)
    halo_copies[1].wait_recv()
    add_halo(ctx_g, 1, wg, GRU_WIDTH)
    add_halo(ctx_c, 1, wc, GRU_WIDTH)
    state = gst[0].reshape(pixels, GRU_WIDTH).astype(F32)
    state_stage = 0
    for iteration in range(ITERS):
        acc_g[...] = ctx_g[...] + interior_conv(state, wg, 0, columns)
        halo_copies[state_stage].wait_recv()
        add_halo(acc_g, state_stage, wg, 0)
        reset = jax.nn.sigmoid(acc_g[:, GRU_WIDTH:])
        reset_state = (reset * state).astype(BF16)
        share_edge(2 + 2 * iteration, reset_state)
        update = jax.nn.sigmoid(acc_g[:, :GRU_WIDTH])
        acc_c[...] = ctx_c[...] + interior_conv(reset_state.astype(F32), wc, 0, columns)
        halo_copies[2 + 2 * iteration].wait_recv()
        add_halo(acc_c, 2 + 2 * iteration, wc, 0)
        candidate = jnp.tanh(acc_c[...])
        new_state = ((1.0 - update) * state + update * candidate).astype(BF16)
        if iteration < ITERS - 1:
            state_stage = 3 + 2 * iteration
            share_edge(state_stage, new_state)
            state = new_state.astype(F32)
    out_state[...] = new_state.reshape(1, rows, columns, GRU_WIDTH)

    for copy in own_back:
        copy.wait()
    for copy in back_copies:
        copy.wait_recv()
    for copy in partner_copies + vis_copies + tok_copies + back_copies + halo_copies:
        copy.wait_send()


def finish(state, tok, returned, wto, out_state, out_track):
    out_state[...] = state[...]
    update = dot(returned[...].reshape(tok.shape[1], tok.shape[2]), wto[...])
    out_track[0] = (tok[0].astype(F32) + update).astype(BF16)


def on_device(frames, bands, *args):
    args = list(args)
    args[4] = args[4].reshape(1, -1)
    time_out = args.pop(12)
    pixels, gru_state, tokens, visible = args[:4]
    tracks, channels = tokens.shape[1:]
    mine = tracks // frames
    chunks = 2 if mine % (2 * GROUP) == 0 else 1
    part_rows = mine // chunks
    rows, columns = pixels.shape[1:3]
    count = rows * columns
    halo_stages = 1 + 2 * ITERS
    dma = pltpu.SemaphoreType.DMA
    scratch = [pltpu.VMEM(a.shape, a.dtype) for a in args] + [
        pltpu.VMEM((tracks, channels), BF16),
        pltpu.VMEM((1, tracks), jnp.int32),
        pltpu.VMEM((chunks, frames, part_rows, channels), BF16),
        pltpu.VMEM((frames, 1, tracks), jnp.int32),
        pltpu.VMEM((count, channels), BF16),
        pltpu.VMEM((tracks, channels), BF16),
        pltpu.VMEM((tracks, channels), BF16),
        pltpu.VMEM((chunks, frames, part_rows, channels), BF16),
        pltpu.VMEM((halo_stages - 1, count, GRU_WIDTH), BF16),
        pltpu.VMEM((halo_stages, columns, GRU_WIDTH), BF16),
        pltpu.VMEM((2, count, channels), F32),
        pltpu.VMEM((2, count, channels), F32),
        pltpu.VMEM((2, count, channels), F32),
        pltpu.VMEM((count, 2 * GRU_WIDTH), F32),
        pltpu.VMEM((count, GRU_WIDTH), F32),
        pltpu.VMEM((count, 2 * GRU_WIDTH), F32),
        pltpu.VMEM((count, GRU_WIDTH), F32),
        dma((N_IN,)),
        dma((chunks + 1,)),
        dma((2,)),
        dma((2,)),
        dma((chunks, frames)),
        dma((chunks, frames)),
        dma((frames,)),
        dma((frames,)),
        dma((chunks, frames)),
        dma((chunks, frames)),
        dma((chunks,)),
        dma((halo_stages,)),
        dma((halo_stages,)),
    ]

    def body(*refs):
        kernel(frames, bands, *refs)

    state, returned = pl.pallas_call(
        body,
        out_shape=(
            jax.ShapeDtypeStruct(gru_state.shape, BF16),
            jax.ShapeDtypeStruct((frames, mine, channels), BF16),
        ),
        in_specs=[pl.BlockSpec(memory_space=pl.ANY)] * N_IN,
        out_specs=(
            pl.BlockSpec(memory_space=pltpu.VMEM),
            pl.BlockSpec(memory_space=pl.ANY),
        ),
        scratch_shapes=scratch,
        compiler_params=pltpu.CompilerParams(collective_id=0, has_side_effects=True),
        name="track_step",
    )(*args)
    return pl.pallas_call(
        finish,
        out_shape=(
            jax.ShapeDtypeStruct(gru_state.shape, BF16),
            jax.ShapeDtypeStruct(tokens.shape, BF16),
        ),
        in_specs=[pl.BlockSpec(memory_space=pltpu.VMEM)] * 4,
        out_specs=(pl.BlockSpec(memory_space=pltpu.VMEM),) * 2,
        name="track_finish",
    )(state, tokens, returned, time_out)


def solution(mesh):
    frames, bands = mesh.shape["frame"], mesh.shape["band"]
    placed = (
        P(("clip", "frame"), "band", None, None),
        P(("clip", "frame"), "band", None, None),
        P(("clip", "frame"), "band", None),
        P(("clip", "frame"), "band"),
        P(("clip", "band")),
    ) + (P(),) * 10
    return jax.shard_map(
        lambda *args: on_device(frames, bands, *args),
        mesh=mesh,
        in_specs=placed,
        out_specs=(P(("clip", "frame"), "band", None, None), P(("clip", "frame"), "band", None)),
        check_vma=False,
    )
```
